512 devices in a mesh: dom: 64 (over z_lo, y, core), head: 8 (over z_hi, x).
Axes of the slice: x: 4, y: 8, z: 8 (z_hi: 2, z_lo: 4; z = z_hi * 4 + z_lo), core: 2. Of those that a mesh axis runs over, the one named last changes fastest.
Arguments:
- node_feats: bfloat16 [24576, 512], P('dom', 'head'), may hold values from -16 to 16
- tile_vals: bfloat16 [192, 4, 128, 128], P('dom'), may hold values from -0.375 to 0.375
- tile_counts: int32 [192], P('dom'), may hold values from 1 to 4
- tile_cols: int32 [192, 4], P('dom'), may hold values from 0 to 6
- send_rows: int32 [64, 4, 128], P('dom'), may hold values from 0 to 383, as said below
- w_msg: bfloat16 [512, 512], P(None, 'head'), may hold values from -0.25 to 0.25
- w_qkv: bfloat16 [3, 512, 512], P(None, None, 'head'), may hold values from -0.25 to 0.25
- w_out: bfloat16 [512, 512], P('head'), may hold values from -0.25 to 0.25
Outputs:
- updated: bfloat16 [24576, 512], P('dom', 'head')
The draws below stay inside these ranges and needn't reach their ends.
Inputs may be any that keep to these rules, and one draw needn't show every extreme that they name: `send_rows`: local row indices within the sending partition. `tile_cols`: block c < 3 of a partition's row table is its own row block c; block 3 + j is the block of 128 rows received with offset index j.
All inputs are finite; a program needn't handle non-finite values.
Results may differ from the reference program's by a relative error of at most 0.012.
The reference program's roundings to bfloat16 on the way count: a program that leaves them out, or rounds other values in their place, can miss the bound.
Values may be sent and summed in bfloat16 or wider, within the bound.
No kernel may reach another device: no remote copies, remote signals or barrier semaphores. Data moves between devices by JAX's collectives and lax.ppermute only.
A program may use at most 64 MiB of HBM per device.

```python
import math
import jax
import jax.numpy as jnp
from jax import lax

D = 512
H = 8
DH = 64
BLK = 128
NODE_DEV = 384
BND = 128
REACH = 2
TPR = 4
RB = 3
EXT_BLK = 7
NODES = 24576
NB = 192
N_DOM = 64


def draw_node_feats(key, part):
    keys_all = jax.random.split(jax.random.fold_in(key, 11), 8)
    part_means = jax.random.normal(keys_all[6], (N_DOM, 1, D), jnp.float32)
    part_scales = jnp.exp(jax.random.uniform(keys_all[7], (N_DOM, 1, 1), jnp.float32, jnp.log(0.5), jnp.log(1.8)))
    noise = jnp.clip(jax.random.normal(keys_all[0], (NODES, D), jnp.float32), -6.0, 6.0) * 0.7
    base = ((noise.reshape(N_DOM, NODE_DEV, D) + part_means) * part_scales).reshape(NODES, D)
    base = jnp.clip(base, -16.0, 16.0)
    return base.astype(jnp.bfloat16)


def draw_send_rows(key, part):
    keys_all = jax.random.split(jax.random.fold_in(key, 23), 3)
    total = N_DOM * 2 * REACH * BND
    flat = jax.random.randint(keys_all[0], (total,), 0, NODE_DEV)
    lower_at = jax.random.randint(keys_all[1], (), 0, total // 2)
    upper_at = jax.random.randint(keys_all[2], (), total // 2, total)
    flat = flat.at[lower_at].set(0).at[upper_at].set(NODE_DEV - 1)
    return flat.reshape(N_DOM, 2 * REACH, BND).astype(jnp.int32)


def with_ends(entries, rng, smallest, largest):
    longest = entries.shape.index(max(entries.shape))
    spots = []
    for shift in (0, 1):
        where = [jax.random.randint(jax.random.fold_in(rng, axis), (), 0, length) for axis, length in enumerate(entries.shape)]
        where[longest] = (where[longest] + shift) % entries.shape[longest]
        spots.append(tuple(where))
    return entries.at[spots[0]].set(smallest).at[spots[1]].set(largest)


def steps_of(stream_key, shape, shards, low, high):
    def one(dim, blocks):
        heights = jax.random.uniform(jax.random.fold_in(jax.random.fold_in(stream_key, 6), dim), (blocks,), jnp.float32, low / len(shards), high / len(shards))
        return jnp.repeat(jnp.exp(heights), shape[dim] // blocks).reshape((-1,) + (1,) * (len(shape) - dim - 1))

    factor_of = one(*shards[0])
    for cut in shards[1:]:
        factor_of = factor_of * one(*cut)
    return factor_of


def bell_draw(key, extent, spread, bound, shards=(), kind=jnp.bfloat16):
    array = jax.random.normal(key, extent, jnp.float32) * spread
    if len(shards) > 0:
        array = steps_of(key, extent, shards, -0.22, 0.18) * array
    return jnp.clip(array, min=-bound, max=bound).astype(kind)


def setup_inputs(seed: int = 0) -> dict:
    seeds = jax.random.split(jax.random.key(seed), 9)
    node_feats = draw_node_feats(jax.random.fold_in(seeds[8], 71), 0)
    tile_vals = bell_draw(seeds[1], (NB, TPR, BLK, BLK), (2 * BLK) ** -0.5, 0.375, ((0, 64),))
    tile_counts = with_ends(jax.random.randint(seeds[2], (NB,), 1, TPR + 1), jax.random.fold_in(seeds[2], 1), 1, TPR).astype(jnp.int32)
    tile_cols = with_ends(jax.random.randint(seeds[3], (NB, TPR), 0, EXT_BLK), jax.random.fold_in(seeds[3], 1), 0, EXT_BLK - 1).astype(jnp.int32)
    send_rows = draw_send_rows(jax.random.fold_in(seeds[8], 71), 0)
    w_msg = bell_draw(seeds[5], (D, D), D ** -0.5, 0.25, ((1, 8),))
    w_qkv = bell_draw(seeds[6], (3, D, D), D ** -0.5, 0.25, ((2, 8),))
    w_out = bell_draw(seeds[7], (D, D), D ** -0.5, 0.25, ((0, 8),))
    return {"node_feats": node_feats, "tile_vals": tile_vals, "tile_counts": tile_counts, "tile_cols": tile_cols, "send_rows": send_rows, "w_msg": w_msg, "w_qkv": w_qkv, "w_out": w_out}


def offsets(reach_count):
    return [position - reach_count if position < reach_count else position - reach_count + 1 for position in range(2 * reach_count)]

def reference(node_feats, tile_vals, tile_counts, tile_cols, send_rows, w_msg, w_qkv, w_out):
    partitions = node_feats.reshape(N_DOM, NODE_DEV, D)
    owners = jnp.arange(N_DOM, dtype=jnp.int32)
    pieces = [partitions]
    for direction, shift_by in enumerate(offsets(REACH)):
        source = ((owners - shift_by) % N_DOM).astype(jnp.int32)
        chosen = partitions[source[:, None], send_rows[source, direction]]
        pieces.append(chosen)
    tables = jnp.concatenate(pieces, axis=1).reshape(N_DOM, EXT_BLK, BLK, D)
    tiles = tile_vals.reshape(N_DOM, RB, TPR, BLK, BLK)
    counts = tile_counts.reshape(N_DOM, RB)
    columns = tile_cols.reshape(N_DOM, RB, TPR)

    def one_part(operands):
        blocks, part_tiles, part_counts, part_cols = operands
        picked = blocks[part_cols].astype(jnp.float32)
        slots = jnp.arange(TPR, dtype=jnp.int32)
        live = slots[None, :] < part_counts[:, None]
        masked = jnp.where(live[:, :, None, None], part_tiles.astype(jnp.float32), jnp.zeros_like(part_tiles, dtype=jnp.float32))
        return jnp.einsum('rtij,rtjc->ric', masked, picked).reshape(NODE_DEV, D)
    aggregated = lax.map(one_part, (tables, tiles, counts, columns)).reshape(NODES, D).astype(jnp.bfloat16)
    message = jnp.maximum(jnp.dot(aggregated, w_msg, preferred_element_type=jnp.float32), 0.0)
    query = jnp.dot(node_feats, w_qkv[0], preferred_element_type=jnp.float32).astype(jnp.bfloat16)
    keys = jnp.dot(node_feats, w_qkv[1], preferred_element_type=jnp.float32).astype(jnp.bfloat16)
    values = jnp.dot(node_feats, w_qkv[2], preferred_element_type=jnp.float32).astype(jnp.bfloat16)
    scale = 1.0 / math.sqrt(DH)
    query_block = math.gcd(NODES, 1024)

    def one_head(operands):
        head_q, head_k, head_v = operands

        def one_block(block_q):
            scores = jnp.dot(block_q, head_k.T, preferred_element_type=jnp.float32) * scale
            weights = jnp.exp(scores - scores.max(axis=1, keepdims=True)).astype(jnp.bfloat16)
            total = weights.astype(jnp.float32).sum(axis=1, keepdims=True)
            return (jnp.dot(weights, head_v, preferred_element_type=jnp.float32) / total).astype(jnp.bfloat16)
        return lax.map(one_block, head_q.reshape(NODES // query_block, query_block, DH)).reshape(NODES, DH)
    split_q = query.reshape(NODES, H, DH).transpose(1, 0, 2)
    split_k = keys.reshape(NODES, H, DH).transpose(1, 0, 2)
    split_v = values.reshape(NODES, H, DH).transpose(1, 0, 2)
    heads_out = lax.map(one_head, (split_q, split_k, split_v)).transpose(1, 0, 2).reshape(NODES, D)
    attended = jnp.dot(heads_out, w_out, preferred_element_type=jnp.float32)
    return (node_feats.astype(jnp.float32) + message + attended).astype(jnp.bfloat16)
```

```python
import math

import jax
import jax.numpy as jnp
from jax import lax
from jax.experimental import pallas as pl
from jax.experimental.pallas import tpu as pltpu
from jax.sharding import Mesh
from jax.sharding import PartitionSpec as P

D = 512
H = 8
DH = D // H
REACH = 2
DOM = ("zl", "y", "c")
HEAD = ("zh", "x")
PARTS = (4, 8, 2, 2, 4)
CARRY = DH + 8
TILE_Q = 256
TILE_K = 512
INTERPRET = False


def offsets(reach_count):
    return [
        position - reach_count if position < reach_count else position - reach_count + 1
        for position in range(2 * reach_count)
    ]


def passed_along(block, axis, distance):
    size = lax.axis_size(axis)
    return lax.ppermute(block, axis, [((i - distance) % size, i) for i in range(size)])


def sent_to_all(block, axis):
    size = lax.axis_size(axis)
    return lax.all_to_all(jnp.broadcast_to(block, (size,) + block.shape), axis, 0, 0)


def matmul(a, b, contract):
    return lax.dot_general(a, b, ((contract[0], contract[1]), ((), ())), preferred_element_type=jnp.float32)


def call(body, outs, scratch=(), smem=(), count=0, flops=0):
    specs = [
        pl.BlockSpec(memory_space=pltpu.SMEM if i in smem else pltpu.VMEM) for i in range(count)
    ]
    outputs = [jax.ShapeDtypeStruct(shape, dtype) for shape, dtype in outs]
    return pl.pallas_call(
        body,
        out_shape=outputs if len(outputs) > 1 else outputs[0],
        in_specs=specs,
        out_specs=[pl.BlockSpec(memory_space=pltpu.VMEM) for _ in outs]
        if len(outputs) > 1
        else pl.BlockSpec(memory_space=pltpu.VMEM),
        scratch_shapes=scratch,
        compiler_params=pltpu.CompilerParams(vmem_limit_bytes=48 * 1024 * 1024),
        cost_estimate=pl.CostEstimate(flops=flops, bytes_accessed=2000000, transcendentals=0),
        interpret=INTERPRET,
    )


def project_body(quad, weights, rows, q_out, kv_out, x_out, *chosen):
    per_z, per_x = quad.shape[1], quad.shape[0]
    for z in range(per_z):
        for x in range(per_x):
            at = (z * per_x + x) * DH
            x_out[at : at + DH, :] = quad[x, z]
    full = x_out[...]
    qkv = matmul(weights[...], full, ((1,), (0,)))
    q_out[...] = (qkv[:DH].astype(jnp.bfloat16).astype(jnp.float32) * (1.0 / math.sqrt(DH))).astype(
        jnp.bfloat16
    )
    kv_out[...] = qkv[DH:].astype(jnp.bfloat16)
    count = full.shape[1]
    for j, out in enumerate(chosen):
        listed = rows[j : j + 1, :]
        spot = lax.broadcasted_iota(jnp.int32, (count, listed.shape[1]), 0) == listed
        out[...] = matmul(full, spot.astype(jnp.bfloat16), ((1,), (0,))).astype(jnp.bfloat16)


def three(value):
    high = value.astype(jnp.bfloat16).astype(jnp.float32)
    rest = value - high
    middle = rest.astype(jnp.bfloat16).astype(jnp.float32)
    return [high, middle, rest - middle]


def attend_body(q, kv_a, kv_b, out, keys, values, queries, scores, results):
    half, _, width = kv_a.shape
    blocks = 2 * half
    for j in range(blocks):
        block = (kv_a if j < half else kv_b)[j % half]
        at = slice(j * width, (j + 1) * width)
        keys[at, :] = block[:DH].T
        values[:DH, at] = block[DH:]
    values[DH:, :] = jnp.ones((CARRY - DH, blocks * width), jnp.bfloat16)
    count = q.shape[0]
    for i in range(count):
        queries[:, i * width : (i + 1) * width] = q[i]
    chunks = blocks * width // TILE_K
    tiles = count * width // TILE_Q

    def score(tile, slot, j):
        at = pl.multiple_of(tile * TILE_Q, TILE_Q)
        part = matmul(keys[j * TILE_K : (j + 1) * TILE_K, :], queries[:, pl.ds(at, TILE_Q)], ((1,), (0,)))
        scores[slot, j * TILE_K : (j + 1) * TILE_K, :] = part
        return part.reshape(TILE_K // 8, 8, TILE_Q).max(axis=0)

    def weigh(slot, j, top):
        part = scores[slot, j * TILE_K : (j + 1) * TILE_K, :]
        weights = jnp.exp(part - top).astype(jnp.bfloat16)
        return matmul(values[:, j * TILE_K : (j + 1) * TILE_K], weights, ((1,), (0,)))

    def finish(tile, total, top):
        sums = total[DH : DH + 1]
        extra = three(top) + three(sums)
        whole = jnp.concatenate([total[:DH]] + extra + [jnp.zeros((2, TILE_Q), jnp.float32)], axis=0)
        at = pl.multiple_of(tile * TILE_Q, TILE_Q)
        results[:, pl.ds(at, TILE_Q)] = whole.astype(jnp.bfloat16)

    def first(slot, tile):
        best = score(tile, slot, 0)
        for j in range(1, chunks):
            best = jnp.maximum(best, score(tile, slot, j))
        return best.max(axis=0, keepdims=True)

    def step(tile, top):
        slot = lax.rem(tile, 2)
        best = None
        total = jnp.zeros((CARRY, TILE_Q), jnp.float32)
        for j in range(chunks):
            part = score(tile + 1, 1 - slot, j)
            best = part if best is None else jnp.maximum(best, part)
            total = total + weigh(slot, j, top)
        finish(tile, total, top)
        return best.max(axis=0, keepdims=True)

    top = lax.fori_loop(0, tiles - 1, step, first(0, 0))
    total = jnp.zeros((CARRY, TILE_Q), jnp.float32)
    for j in range(chunks):
        total = total + weigh((tiles - 1) % 2, j, top)
    finish(tiles - 1, total, top)
    for i in range(count):
        out[i] = results[:, i * width : (i + 1) * width]


def combine_body(parts, w_out, out):
    count = parts.shape[0]
    tail = [parts[i, DH:, :].astype(jnp.float32) for i in range(count)]
    tops = [t[0:1] + t[1:2] + t[2:3] for t in tail]
    sums = [t[3:4] + t[4:5] + t[5:6] for t in tail]
    best = tops[0]
    for top in tops[1:]:
        best = jnp.maximum(best, top)
    total = jnp.zeros_like(best)
    value = jnp.zeros((DH, best.shape[1]), jnp.float32)
    for i in range(count):
        factor = jnp.exp(tops[i] - best)
        total = total + factor * sums[i]
        value = value + factor * parts[i, :DH, :].astype(jnp.float32)
    heads_out = (value / total).astype(jnp.bfloat16)
    for h in range(H):
        share = matmul(w_out[:, h * DH : (h + 1) * DH], heads_out, ((0,), (0,)))
        out[h] = share.astype(jnp.bfloat16)


def message_body(x, r0, r1, r2, r3, tiles, counts, cols, w_msg, out, table):
    own, slots, size, _ = tiles.shape
    for b in range(own):
        table[b] = x[:, b * size : (b + 1) * size]
    for j, received in enumerate((r0, r1, r2, r3)):
        table[own + j] = received[...]
    for r in range(own):
        total = jnp.zeros((D, size), jnp.float32)
        for t in range(slots):
            tile = tiles[r, t]
            tile = jnp.where(t < counts[r], tile, jnp.zeros_like(tile))
            total = total + matmul(table[cols[r, t]], tile, ((1,), (1,)))
        projected = matmul(w_msg[...], total.astype(jnp.bfloat16), ((1,), (0,)))
        out[:, r * size : (r + 1) * size] = jnp.maximum(projected, 0.0)


def local(node_feats, tile_vals, tile_counts, tile_cols, send_rows, w_msg, w_qkv, w_out):
    rows = node_feats.shape[0]
    bf16, f32 = jnp.bfloat16, jnp.float32
    listed = send_rows[0]
    directions, bound = listed.shape
    x_own = node_feats.T
    pair = lax.all_gather(x_own, "zh", axis=0, tiled=False)
    quad = sent_to_all(pair, "x")
    weights = jnp.swapaxes(w_qkv, 1, 2).reshape(3 * DH, D)
    q, kv, x_full, *chosen = call(
        project_body,
        [((DH, rows), bf16), ((2 * DH, rows), bf16), ((D, rows), bf16)] + [((D, bound), bf16)] * directions,
        count=3,
        flops=2 * D * rows * (3 * DH + directions * bound),
    )(quad, weights, listed)
    received = [passed_along(block, DOM, o) for block, o in zip(chosen, offsets(REACH))]
    queries = sent_to_all(q, "y")
    kv_a = sent_to_all(kv, "zl")
    kv_b = passed_along(kv_a, "c", 1)
    keys = 2 * kv_a.shape[0] * rows
    asked = queries.shape[0] * rows
    parts = call(
        attend_body,
        [((queries.shape[0], CARRY, rows), bf16)],
        scratch=[
            pltpu.VMEM((keys, DH), bf16),
            pltpu.VMEM((CARRY, keys), bf16),
            pltpu.VMEM((DH, asked), bf16),
            pltpu.VMEM((2, keys, TILE_Q), f32),
            pltpu.VMEM((CARRY, asked), bf16),
        ],
        count=3,
        flops=4 * DH * keys * asked,
    )(queries, kv_a, kv_b)
    parts = lax.all_to_all(parts, "y", 0, 0)
    shares = call(combine_body, [((H, DH, rows), bf16)], count=2, flops=2 * D * DH * rows)(parts, w_out)
    shares = lax.all_to_all(shares, HEAD, 0, 0)
    message = call(
        message_body,
        [((DH, rows), f32)],
        scratch=[pltpu.VMEM((rows // bound + directions, D, bound), bf16)],
        smem=(6, 7),
        count=9,
        flops=2 * D * rows * (4 * bound + DH),
    )(x_full, *received, tile_vals, tile_counts, tile_cols, w_msg.T)
    attended = shares.astype(f32).sum(axis=0)
    return (x_own.astype(f32) + message + attended).astype(bf16).T


def solution(mesh):
    parts = Mesh(mesh.devices.reshape(PARTS), DOM + HEAD)
    placed = (
        P(DOM, HEAD),
        P(DOM, None, None, None),
        P(DOM),
        P(DOM, None),
        P(DOM, None, None),
        P(None, HEAD),
        P(None, None, HEAD),
        P(HEAD, None),
    )
    return jax.shard_map(local, mesh=parts, in_specs=placed, out_specs=P(DOM, HEAD), check_vma=False)
```

```python
import math

import jax
import jax.numpy as jnp
from jax import lax
from jax.experimental import pallas as pl
from jax.experimental.pallas import tpu as pltpu
from jax.sharding import Mesh
from jax.sharding import PartitionSpec as P


D = 512
H = 8
DH = D // H
REACH = 2
DOM = ("zl", "y", "c")
HEAD = ("zh", "x")
PARTS = (4, 8, 2, 2, 4)
CARRY = DH + 8
TILE_Q = 1024
TILE_K = 512
INTERPRET = False


def offsets(reach_count):
    return [
        position - reach_count if position < reach_count else position - reach_count + 1
        for position in range(2 * reach_count)
    ]


def passed_along(block, axis, distance):
    size = lax.axis_size(axis)
    return lax.ppermute(block, axis, [((i - distance) % size, i) for i in range(size)])


def sent_to_all(block, axis):
    size = lax.axis_size(axis)
    return lax.all_to_all(jnp.broadcast_to(block, (size,) + block.shape), axis, 0, 0)


def matmul(a, b, contract):
    return lax.dot_general(a, b, ((contract[0], contract[1]), ((), ())), preferred_element_type=jnp.float32)


def call(body, outs, scratch=(), smem=(), count=0, flops=0):
    specs = [
        pl.BlockSpec(memory_space=pltpu.SMEM if i in smem else pltpu.VMEM) for i in range(count)
    ]
    outputs = [jax.ShapeDtypeStruct(shape, dtype) for shape, dtype in outs]
    return pl.pallas_call(
        body,
        out_shape=outputs if len(outputs) > 1 else outputs[0],
        in_specs=specs,
        out_specs=[pl.BlockSpec(memory_space=pltpu.VMEM) for _ in outs]
        if len(outputs) > 1
        else pl.BlockSpec(memory_space=pltpu.VMEM),
        scratch_shapes=scratch,
        compiler_params=pltpu.CompilerParams(vmem_limit_bytes=48 * 1024 * 1024),
        cost_estimate=pl.CostEstimate(flops=flops, bytes_accessed=2000000, transcendentals=0),
        interpret=INTERPRET,
    )


def project_body(quad, weights, rows, q_out, kv_out, x_out, *chosen):
    per_z, per_x = quad.shape[1], quad.shape[0]
    for z in range(per_z):
        for x in range(per_x):
            at = (z * per_x + x) * DH
            x_out[at : at + DH, :] = quad[x, z]
    full = x_out[...]
    qkv = matmul(weights[...], full, ((1,), (0,)))
    query = qkv[:DH].astype(jnp.bfloat16).astype(jnp.float32) * (1.0 / math.sqrt(DH))
    for i in range(q_out.shape[0]):
        q_out[i] = query.astype(jnp.bfloat16)
    kv_out[...] = qkv[DH:].astype(jnp.bfloat16)
    count = full.shape[1]
    for j, out in enumerate(chosen):
        listed = rows[j : j + 1, :]
        spot = lax.broadcasted_iota(jnp.int32, (count, listed.shape[1]), 0) == listed
        out[...] = matmul(full, spot.astype(jnp.bfloat16), ((1,), (0,))).astype(jnp.bfloat16)


def three(value):
    high = value.astype(jnp.bfloat16).astype(jnp.float32)
    rest = value - high
    middle = rest.astype(jnp.bfloat16).astype(jnp.float32)
    return [high, middle, rest - middle]


def attend_body(q, kv, out, keys, values, queries, scores, weights, results):
    blocks, _, width = kv.shape
    for j in range(blocks):
        block = kv[j]
        at = slice(j * width, (j + 1) * width)
        keys[at, :] = block[:DH].T
        values[:DH, at] = block[DH:]
    values[DH:, :] = jnp.ones((CARRY - DH, blocks * width), jnp.bfloat16)
    count = q.shape[0]
    for i in range(count):
        queries[:, i * width : (i + 1) * width] = q[i]
    chunks = [slice(j * TILE_K, (j + 1) * TILE_K) for j in range(blocks * width // TILE_K)]

    def step(tile, carried):
        at = pl.multiple_of(tile * TILE_Q, TILE_Q)
        asked = queries[:, pl.ds(at, TILE_Q)]
        best = None
        for chunk in chunks:
            part = matmul(keys[chunk, :], asked, ((1,), (0,)))
            scores[chunk, :] = part
            high = part.reshape(TILE_K // 8, 8, TILE_Q).max(axis=0)
            best = high if best is None else jnp.maximum(best, high)
        top = best.max(axis=0, keepdims=True)
        for chunk in chunks:
            weights[chunk, :] = jnp.exp(scores[chunk, :] - top).astype(jnp.bfloat16)
        total = matmul(values[...], weights[...], ((1,), (0,)))
        rows = [total[:DH]] + three(top) + three(total[DH : DH + 1]) + [jnp.zeros((2, TILE_Q), jnp.float32)]
        results[:, pl.ds(at, TILE_Q)] = jnp.concatenate(rows, axis=0).astype(jnp.bfloat16)
        return carried

    lax.fori_loop(0, count * width // TILE_Q, step, 0)
    for i in range(count):
        out[i] = results[:, i * width : (i + 1) * width]


def combine_body(parts, w_out, out):
    count = parts.shape[0]
    tail = [parts[i, DH:, :].astype(jnp.float32) for i in range(count)]
    tops = [t[0:1] + t[1:2] + t[2:3] for t in tail]
    sums = [t[3:4] + t[4:5] + t[5:6] for t in tail]
    best = tops[0]
    for top in tops[1:]:
        best = jnp.maximum(best, top)
    total = jnp.zeros_like(best)
    value = jnp.zeros((DH, best.shape[1]), jnp.float32)
    for i in range(count):
        factor = jnp.exp(tops[i] - best)
        total = total + factor * sums[i]
        value = value + factor * parts[i, :DH, :].astype(jnp.float32)
    heads_out = (value / total).astype(jnp.bfloat16)
    for h in range(H):
        share = matmul(w_out[:, h * DH : (h + 1) * DH], heads_out, ((0,), (0,)))
        out[h] = share.astype(jnp.bfloat16)


def message_body(x, r0, r1, r2, r3, tiles, counts, cols, w_msg, own_x, out, table):
    own, slots, size, _ = tiles.shape
    for b in range(own):
        table[b] = x[:, b * size : (b + 1) * size]
    for j, received in enumerate((r0, r1, r2, r3)):
        table[own + j] = received[...]
    for r in range(own):
        total = jnp.zeros((D, size), jnp.float32)
        for t in range(slots):
            tile = tiles[r, t]
            tile = jnp.where(t < counts[r], tile, jnp.zeros_like(tile))
            total = total + matmul(table[cols[r, t]], tile, ((1,), (1,)))
        projected = matmul(w_msg[...], total.astype(jnp.bfloat16), ((1,), (0,)))
        at = slice(r * size, (r + 1) * size)
        out[:, at] = own_x[:, at].astype(jnp.float32) + jnp.maximum(projected, 0.0)


def local(node_feats, tile_vals, tile_counts, tile_cols, send_rows, w_msg, w_qkv, w_out):
    rows = node_feats.shape[0]
    bf16, f32 = jnp.bfloat16, jnp.float32
    listed = send_rows[0]
    directions, bound = listed.shape
    askers, givers = lax.axis_size("y"), lax.axis_size(("zl", "c"))
    keys, asked = givers * rows, askers * rows
    x_own = node_feats.T
    pair = lax.all_gather(x_own, "zh", axis=0, tiled=False)
    quad = sent_to_all(pair, "x")
    weights = jnp.swapaxes(w_qkv, 1, 2).reshape(3 * DH, D)
    q, kv, x_full, *chosen = call(
        project_body,
        [((askers, DH, rows), bf16), ((2 * DH, rows), bf16), ((D, rows), bf16)]
        + [((D, bound), bf16)] * directions,
        count=3,
        flops=2 * D * rows * (3 * DH + directions * bound),
    )(quad, weights, listed)
    queries = lax.all_to_all(q, "y", 0, 0)
    held = lax.all_gather(kv, ("zl", "c"), axis=0, tiled=False)
    parts = call(
        attend_body,
        [((askers, CARRY, rows), bf16)],
        scratch=[
            pltpu.VMEM((keys, DH), bf16),
            pltpu.VMEM((CARRY, keys), bf16),
            pltpu.VMEM((DH, asked), bf16),
            pltpu.VMEM((keys, TILE_Q), f32),
            pltpu.VMEM((keys, TILE_Q), bf16),
            pltpu.VMEM((CARRY, asked), bf16),
        ],
        count=2,
        flops=4 * DH * keys * asked,
    )(queries, held)
    parts = lax.all_to_all(parts, "y", 0, 0)
    shares = call(combine_body, [((H, DH, rows), bf16)], count=2, flops=2 * D * DH * rows)(parts, w_out)
    received = [passed_along(block, DOM, o) for block, o in zip(chosen, offsets(REACH))]
    shares = lax.all_to_all(shares, HEAD, 0, 0)
    base = call(
        message_body,
        [((DH, rows), f32)],
        scratch=[pltpu.VMEM((rows // bound + directions, D, bound), bf16)],
        smem=(6, 7),
        count=10,
        flops=2 * D * rows * (4 * bound + DH),
    )(x_full, *received, tile_vals, tile_counts, tile_cols, w_msg.T, x_own)
    return (base + shares.astype(f32).sum(axis=0)).astype(bf16).T


def solution(mesh):
    parts = Mesh(mesh.devices.reshape(PARTS), DOM + HEAD)
    placed = (
        P(DOM, HEAD),
        P(DOM, None, None, None),
        P(DOM),
        P(DOM, None),
        P(DOM, None, None),
        P(None, HEAD),
        P(None, None, HEAD),
        P(HEAD, None),
    )
    return jax.shard_map(local, mesh=parts, in_specs=placed, out_specs=P(DOM, HEAD), check_vma=False)
```

```python
import math

import jax
import jax.numpy as jnp
from jax import lax
from jax.experimental import pallas as pl
from jax.experimental.pallas import tpu as pltpu
from jax.sharding import Mesh
from jax.sharding import PartitionSpec as P


D = 512
H = 8
DH = D // H
REACH = 2
DOM = ("zl", "y", "c")
HEAD = ("zh", "x")
PARTS = (4, 8, 2, 2, 4)
CARRY = DH + 8
TILE_Q = 256
TILE_K = 256
INTERPRET = False


def offsets(reach_count):
    return [
        position - reach_count if position < reach_count else position - reach_count + 1
        for position in range(2 * reach_count)
    ]


def passed_along(block, axis, distance):
    size = lax.axis_size(axis)
    return lax.ppermute(block, axis, [((i - distance) % size, i) for i in range(size)])


def sent_to_all(block, axis):
    size = lax.axis_size(axis)
    return lax.all_to_all(jnp.broadcast_to(block, (size,) + block.shape), axis, 0, 0)


def matmul(a, b, contract):
    return lax.dot_general(a, b, ((contract[0], contract[1]), ((), ())), preferred_element_type=jnp.float32)


def call(body, outs, scratch=(), smem=(), count=0, flops=0):
    specs = [
        pl.BlockSpec(memory_space=pltpu.SMEM if i in smem else pltpu.VMEM) for i in range(count)
    ]
    outputs = [jax.ShapeDtypeStruct(shape, dtype) for shape, dtype in outs]
    return pl.pallas_call(
        body,
        out_shape=outputs if len(outputs) > 1 else outputs[0],
        in_specs=specs,
        out_specs=[pl.BlockSpec(memory_space=pltpu.VMEM) for _ in outs]
        if len(outputs) > 1
        else pl.BlockSpec(memory_space=pltpu.VMEM),
        scratch_shapes=scratch,
        compiler_params=pltpu.CompilerParams(vmem_limit_bytes=48 * 1024 * 1024),
        cost_estimate=pl.CostEstimate(flops=flops, bytes_accessed=2000000, transcendentals=0),
        interpret=INTERPRET,
    )


def project_body(quad, weights, q_out, kv_out, x_out):
    per_z, per_x = quad.shape[1], quad.shape[0]
    for z in range(per_z):
        for x in range(per_x):
            at = (z * per_x + x) * DH
            x_out[at : at + DH, :] = quad[x, z]
    full = x_out[...]
    qkv = matmul(weights[...], full, ((1,), (0,)))
    query = qkv[:DH].astype(jnp.bfloat16).astype(jnp.float32) * (1.0 / math.sqrt(DH))
    for i in range(q_out.shape[0]):
        q_out[i] = query.astype(jnp.bfloat16)
    kv_out[...] = qkv[DH:].astype(jnp.bfloat16)


def choose_body(x, rows, *chosen):
    for j, out in enumerate(chosen):
        listed = rows[j : j + 1, :]
        spot = lax.broadcasted_iota(jnp.int32, (x.shape[1], listed.shape[1]), 0) == listed
        out[...] = matmul(x[...], spot.astype(jnp.bfloat16), ((1,), (0,))).astype(jnp.bfloat16)


def three(value):
    high = value.astype(jnp.bfloat16).astype(jnp.float32)
    rest = value - high
    middle = rest.astype(jnp.bfloat16).astype(jnp.float32)
    return [high, middle, rest - middle]


def attend_body(q, kv, out, keys, values, queries, scores_a, scores_b, weights_a, weights_b, results):
    blocks, _, width = kv.shape
    for j in range(blocks):
        at = slice(j * width, (j + 1) * width)
        keys[at, :] = kv[j, :DH].T
        values[:DH, at] = kv[j, DH:]
    values[DH:, :] = jnp.ones((CARRY - DH, blocks * width), jnp.bfloat16)
    count = q.shape[0]
    for i in range(count):
        queries[:, i * width : (i + 1) * width] = q[i]
    chunks = [slice(j * TILE_K, (j + 1) * TILE_K) for j in range(blocks * width // TILE_K)]
    tiles = count * width // TILE_Q

    def score(asked, scores, chunk, best):
        part = matmul(keys[chunk, :], asked, ((1,), (0,)))
        scores[chunk, :] = part
        high = part.reshape(TILE_K // 8, 8, TILE_Q).max(axis=0)
        return high if best is None else jnp.maximum(best, high)

    def half(tile, scores, scores_next, weights, top):
        following = pl.multiple_of(jnp.minimum(tile + 1, tiles - 1) * TILE_Q, TILE_Q)
        asked = queries[:, pl.ds(following, TILE_Q)]
        best = None
        for chunk in chunks:
            weights[chunk, :] = jnp.exp(scores[chunk, :] - top).astype(jnp.bfloat16)
            best = score(asked, scores_next, chunk, best)
        total = matmul(values[...], weights[...], ((1,), (0,)))
        rows = [total[:DH]] + three(top) + three(total[DH : DH + 1]) + [jnp.zeros((2, TILE_Q), jnp.float32)]
        at = pl.multiple_of(tile * TILE_Q, TILE_Q)
        results[:, pl.ds(at, TILE_Q)] = jnp.concatenate(rows, axis=0).astype(jnp.bfloat16)
        return best.max(axis=0, keepdims=True)

    def step(pair, top):
        top = half(2 * pair, scores_a, scores_b, weights_a, top)
        return half(2 * pair + 1, scores_b, scores_a, weights_b, top)

    best = None
    for chunk in chunks:
        best = score(queries[:, :TILE_Q], scores_a, chunk, best)
    lax.fori_loop(0, tiles // 2, step, best.max(axis=0, keepdims=True))
    for i in range(count):
        out[i] = results[:, i * width : (i + 1) * width]


def combine_body(parts, w_out, out):
    count = parts.shape[0]
    tail = [parts[i, DH:, :].astype(jnp.float32) for i in range(count)]
    tops = [t[0:1] + t[1:2] + t[2:3] for t in tail]
    sums = [t[3:4] + t[4:5] + t[5:6] for t in tail]
    best = tops[0]
    for top in tops[1:]:
        best = jnp.maximum(best, top)
    total = jnp.zeros_like(best)
    value = jnp.zeros((DH, best.shape[1]), jnp.float32)
    for i in range(count):
        factor = jnp.exp(tops[i] - best)
        total = total + factor * sums[i]
        value = value + factor * parts[i, :DH, :].astype(jnp.float32)
    heads_out = (value / total).astype(jnp.bfloat16)
    for h in range(H):
        share = matmul(w_out[:, h * DH : (h + 1) * DH], heads_out, ((0,), (0,)))
        out[h] = share.astype(jnp.bfloat16)


def message_body(x, r0, r1, r2, r3, tiles, counts, cols, w_msg, own_x, out, table):
    own, slots, size, _ = tiles.shape
    for b in range(own):
        table[b] = x[:, b * size : (b + 1) * size]
    for j, received in enumerate((r0, r1, r2, r3)):
        table[own + j] = received[...]
    for r in range(own):
        total = jnp.zeros((D, size), jnp.float32)
        for t in range(slots):
            tile = tiles[r, t]
            tile = jnp.where(t < counts[r], tile, jnp.zeros_like(tile))
            total = total + matmul(table[cols[r, t]], tile, ((1,), (1,)))
        projected = matmul(w_msg[...], total.astype(jnp.bfloat16), ((1,), (0,)))
        at = slice(r * size, (r + 1) * size)
        out[:, at] = own_x[:, at].astype(jnp.float32) + jnp.maximum(projected, 0.0)


def local(node_feats, tile_vals, tile_counts, tile_cols, send_rows, w_msg, w_qkv, w_out):
    rows = node_feats.shape[0]
    bf16, f32 = jnp.bfloat16, jnp.float32
    listed = send_rows[0]
    directions, bound = listed.shape
    askers, givers = lax.axis_size("y"), lax.axis_size(("zl", "c"))
    keys, asked = givers * rows, askers * rows
    x_own = node_feats.T
    pair = lax.all_gather(x_own, "zh", axis=0, tiled=False)
    quad = sent_to_all(pair, "x")
    weights = jnp.swapaxes(w_qkv, 1, 2).reshape(3 * DH, D)
    q, kv, x_full = call(
        project_body,
        [((askers, DH, rows), bf16), ((2 * DH, rows), bf16), ((D, rows), bf16)],
        count=2,
        flops=2 * D * rows * 3 * DH,
    )(quad, weights)
    queries = lax.all_to_all(q, "y", 0, 0)
    held = lax.all_gather(kv, ("zl", "c"), axis=0, tiled=False)
    parts = call(
        attend_body,
        [((askers, CARRY, rows), bf16)],
        scratch=[
            pltpu.VMEM((keys, DH), bf16),
            pltpu.VMEM((CARRY, keys), bf16),
            pltpu.VMEM((DH, asked), bf16),
            pltpu.VMEM((keys, TILE_Q), f32),
            pltpu.VMEM((keys, TILE_Q), f32),
            pltpu.VMEM((keys, TILE_Q), bf16),
            pltpu.VMEM((keys, TILE_Q), bf16),
            pltpu.VMEM((CARRY, asked), bf16),
        ],
        count=2,
        flops=4 * DH * keys * asked,
    )(queries, held)
    parts = lax.all_to_all(parts, "y", 0, 0)
    shares = call(combine_body, [((H, DH, rows), bf16)], count=2, flops=2 * D * DH * rows)(parts, w_out)
    chosen = call(
        choose_body,
        [((D, bound), bf16)] * directions,
        count=2,
        flops=2 * D * rows * directions * bound,
    )(x_full, listed)
    received = []
    for block, offset in zip(chosen, offsets(REACH)):
        received.append(passed_along(block, DOM, offset))
    shares = lax.all_to_all(shares, HEAD, 0, 0)
    base = call(
        message_body,
        [((DH, rows), f32)],
        scratch=[pltpu.VMEM((rows // bound + directions, D, bound), bf16)],
        smem=(6, 7),
        count=10,
        flops=2 * D * rows * (4 * bound + DH),
    )(x_full, *received, tile_vals, tile_counts, tile_cols, w_msg.T, x_own)
    return (base + shares.astype(f32).sum(axis=0)).astype(bf16).T


def solution(mesh):
    parts = Mesh(mesh.devices.reshape(PARTS), DOM + HEAD)
    placed = (
        P(DOM, HEAD),
        P(DOM, None, None, None),
        P(DOM),
        P(DOM, None),
        P(DOM, None, None),
        P(None, HEAD),
        P(None, None, HEAD),
        P(HEAD, None),
    )
    return jax.shard_map(local, mesh=parts, in_specs=placed, out_specs=P(DOM, HEAD), check_vma=False)
```

```python
import math

import jax
import jax.numpy as jnp
from jax import lax
from jax.experimental import pallas as pl
from jax.experimental.pallas import tpu as pltpu
from jax.sharding import Mesh
from jax.sharding import PartitionSpec as P


D = 512
H = 8
DH = D // H
REACH = 2
DOM = ("zl", "y", "c")
HEAD = ("zh", "x")
PARTS = (4, 8, 2, 2, 4)
CARRY = DH + 8
TILE_Q = 256
TILE_K = 256
INTERPRET = False


def passed_along(block, axis, distance):
    size = lax.axis_size(axis)
    return lax.ppermute(block, axis, [((i - distance) % size, i) for i in range(size)])


def sent_to_all(block, axis):
    size = lax.axis_size(axis)
    return lax.all_to_all(jnp.broadcast_to(block, (size,) + block.shape), axis, 0, 0)


def matmul(a, b, contract):
    return lax.dot_general(a, b, ((contract[0], contract[1]), ((), ())), preferred_element_type=jnp.float32)


def call(body, outs, scratch=(), smem=(), hbm=(), count=0, flops=0):
    specs = [
        pl.BlockSpec(memory_space=pltpu.SMEM if i in smem else pltpu.HBM if i in hbm else pltpu.VMEM)
        for i in range(count)
    ]
    outputs = [jax.ShapeDtypeStruct(shape, dtype) for shape, dtype in outs]
    return pl.pallas_call(
        body,
        out_shape=outputs if len(outputs) > 1 else outputs[0],
        in_specs=specs,
        out_specs=[pl.BlockSpec(memory_space=pltpu.VMEM) for _ in outs]
        if len(outputs) > 1
        else pl.BlockSpec(memory_space=pltpu.VMEM),
        scratch_shapes=scratch,
        compiler_params=pltpu.CompilerParams(vmem_limit_bytes=48 * 1024 * 1024),
        cost_estimate=pl.CostEstimate(flops=flops, bytes_accessed=2000000, transcendentals=0),
        interpret=INTERPRET,
    )


def project_body(quad, weights, q_out, kv_out, x_out):
    per_z, per_x = quad.shape[1], quad.shape[0]
    for z in range(per_z):
        for x in range(per_x):
            at = (z * per_x + x) * DH
            x_out[at : at + DH, :] = quad[x, z]
    full = x_out[...]
    qkv = matmul(weights[...], full, ((1,), (0,)))
    query = qkv[:DH].astype(jnp.bfloat16).astype(jnp.float32) * (1.0 / math.sqrt(DH))
    for i in range(q_out.shape[0]):
        q_out[i] = query.astype(jnp.bfloat16)
    kv_out[...] = qkv[DH:].astype(jnp.bfloat16)


def three(value):
    high = value.astype(jnp.bfloat16).astype(jnp.float32)
    rest = value - high
    middle = rest.astype(jnp.bfloat16).astype(jnp.float32)
    return [high, middle, rest - middle]


def attend_body(q, kv, x, rows, out, down, up, partner, cross, keys, values, queries, scores_a, scores_b, weights_a, weights_b, results, lists, arrived):
    fetch = pltpu.make_async_copy(rows, lists, arrived)
    fetch.start()
    blocks, _, width = kv.shape
    for j in range(blocks):
        at = slice(j * width, (j + 1) * width)
        keys[at, :] = kv[j, :DH].T
        values[:DH, at] = kv[j, DH:]
    values[DH:, :] = jnp.ones((CARRY - DH, blocks * width), jnp.bfloat16)
    count = q.shape[0]
    for i in range(count):
        queries[:, i * width : (i + 1) * width] = q[i]
    chunks = [slice(j * TILE_K, (j + 1) * TILE_K) for j in range(blocks * width // TILE_K)]
    tiles = count * width // TILE_Q

    def score(asked, scores, chunk, best):
        part = matmul(keys[chunk, :], asked, ((1,), (0,)))
        scores[chunk, :] = part
        high = part.reshape(TILE_K // 8, 8, TILE_Q).max(axis=0)
        return high if best is None else jnp.maximum(best, high)

    def half(tile, scores, scores_next, weights, top):
        following = pl.multiple_of(jnp.minimum(tile + 1, tiles - 1) * TILE_Q, TILE_Q)
        asked = queries[:, pl.ds(following, TILE_Q)]
        best = None
        for chunk in chunks:
            weights[chunk, :] = jnp.exp(scores[chunk, :] - top).astype(jnp.bfloat16)
            best = score(asked, scores_next, chunk, best)
        total = matmul(values[...], weights[...], ((1,), (0,)))
        rows = [total[:DH]] + three(top) + three(total[DH : DH + 1]) + [jnp.zeros((2, TILE_Q), jnp.float32)]
        at = pl.multiple_of(tile * TILE_Q, TILE_Q)
        results[:, pl.ds(at, TILE_Q)] = jnp.concatenate(rows, axis=0).astype(jnp.bfloat16)
        return best.max(axis=0, keepdims=True)

    def step(pair, top):
        top = half(2 * pair, scores_a, scores_b, weights_a, top)
        return half(2 * pair + 1, scores_b, scores_a, weights_b, top)

    best = None
    for chunk in chunks:
        best = score(queries[:, :TILE_Q], scores_a, chunk, best)
    lax.fori_loop(0, tiles // 2, step, best.max(axis=0, keepdims=True))
    for i in range(count):
        out[i] = results[:, i * width : (i + 1) * width]
    fetch.wait()
    core = lax.axis_index("c")
    for j, chosen in ((0, down), (2 * REACH - 1, up), (REACH - core, partner), (REACH - 1 + core, cross)):
        listed = lists[pl.ds(j, 1), :]
        spot = lax.broadcasted_iota(jnp.int32, (x.shape[1], listed.shape[1]), 0) == listed
        chosen[...] = matmul(x[...], spot.astype(jnp.bfloat16), ((1,), (0,))).astype(jnp.bfloat16)


def combine_body(parts, w_out, out):
    count = parts.shape[0]
    tail = [parts[i, DH:, :].astype(jnp.float32) for i in range(count)]
    tops = [t[0:1] + t[1:2] + t[2:3] for t in tail]
    sums = [t[3:4] + t[4:5] + t[5:6] for t in tail]
    best = tops[0]
    for top in tops[1:]:
        best = jnp.maximum(best, top)
    total = jnp.zeros_like(best)
    value = jnp.zeros((DH, best.shape[1]), jnp.float32)
    for i in range(count):
        factor = jnp.exp(tops[i] - best)
        total = total + factor * sums[i]
        value = value + factor * parts[i, :DH, :].astype(jnp.float32)
    heads_out = (value / total).astype(jnp.bfloat16)
    for h in range(H):
        share = matmul(w_out[:, h * DH : (h + 1) * DH], heads_out, ((0,), (0,)))
        out[h] = share.astype(jnp.bfloat16)


def message_body(x, down, up, partner, cross, tiles, counts, cols, w_msg, own_x, out, table):
    own, slots, size, _ = tiles.shape
    for b in range(own):
        table[b] = x[:, b * size : (b + 1) * size]
    core = lax.axis_index("c")
    for j, received in ((0, down), (2 * REACH - 1, up), (REACH - 1 + core, partner), (REACH - core, cross)):
        table[own + j] = received[...]
    for r in range(own):
        total = jnp.zeros((D, size), jnp.float32)
        for t in range(slots):
            tile = tiles[r, t]
            tile = jnp.where(t < counts[r], tile, jnp.zeros_like(tile))
            total = total + matmul(table[cols[r, t]], tile, ((1,), (1,)))
        projected = matmul(w_msg[...], total.astype(jnp.bfloat16), ((1,), (0,)))
        at = slice(r * size, (r + 1) * size)
        out[:, at] = own_x[:, at].astype(jnp.float32) + jnp.maximum(projected, 0.0)


def local(node_feats, tile_vals, tile_counts, tile_cols, send_rows, w_msg, w_qkv, w_out):
    rows = node_feats.shape[0]
    bf16, f32 = jnp.bfloat16, jnp.float32
    listed = send_rows[0]
    directions, bound = listed.shape
    askers, givers = lax.axis_size("y"), lax.axis_size(("zl", "c"))
    keys, asked = givers * rows, askers * rows
    x_own = node_feats.T
    pair = lax.all_gather(x_own, "zh", axis=0, tiled=False)
    quad = sent_to_all(pair, "x")
    weights = jnp.swapaxes(w_qkv, 1, 2).reshape(3 * DH, D)
    q, kv, x_full = call(
        project_body,
        [((askers, DH, rows), bf16), ((2 * DH, rows), bf16), ((D, rows), bf16)],
        count=2,
        flops=2 * D * rows * 3 * DH,
    )(quad, weights)
    queries = lax.all_to_all(q, "y", 0, 0)
    held = lax.all_gather(kv, ("zl", "c"), axis=0, tiled=False)
    parts, down, up, partner, cross = call(
        attend_body,
        [((askers, CARRY, rows), bf16)] + [((D, bound), bf16)] * directions,
        scratch=[
            pltpu.VMEM((keys, DH), bf16),
            pltpu.VMEM((CARRY, keys), bf16),
            pltpu.VMEM((DH, asked), bf16),
            pltpu.VMEM((keys, TILE_Q), f32),
            pltpu.VMEM((keys, TILE_Q), f32),
            pltpu.VMEM((keys, TILE_Q), bf16),
            pltpu.VMEM((keys, TILE_Q), bf16),
            pltpu.VMEM((CARRY, asked), bf16),
            pltpu.VMEM((directions, bound), jnp.int32),
            pltpu.SemaphoreType.DMA,
        ],
        hbm=(3,),
        count=4,
        flops=4 * DH * keys * asked,
    )(queries, held, x_full, listed)
    parts = lax.all_to_all(parts, "y", 0, 0)
    shares = call(combine_body, [((H, DH, rows), bf16)], count=2, flops=2 * D * DH * rows)(parts, w_out)
    down = passed_along(down, DOM, -REACH)
    up = passed_along(up, DOM, REACH)
    size = lax.axis_size(DOM)
    cross = lax.ppermute(cross, DOM, [(i, (i + (1 if i % 2 else -1)) % size) for i in range(size)])
    partner = passed_along(partner, "c", 1)
    shares = lax.all_to_all(shares, HEAD, 0, 0)
    base = call(
        message_body,
        [((DH, rows), f32)],
        scratch=[pltpu.VMEM((rows // bound + directions, D, bound), bf16)],
        smem=(6, 7),
        count=10,
        flops=2 * D * rows * (4 * bound + DH),
    )(x_full, down, up, partner, cross, tile_vals, tile_counts, tile_cols, w_msg.T, x_own)
    return (base + shares.astype(f32).sum(axis=0)).astype(bf16).T


def solution(mesh):
    parts = Mesh(mesh.devices.reshape(PARTS), DOM + HEAD)
    placed = (
        P(DOM, HEAD),
        P(DOM, None, None, None),
        P(DOM),
        P(DOM, None),
        P(DOM, None, None),
        P(None, HEAD),
        P(None, None, HEAD),
        P(HEAD, None),
    )
    return jax.shard_map(local, mesh=parts, in_specs=placed, out_specs=P(DOM, HEAD), check_vma=False)
```

```python
import math

import jax
import jax.numpy as jnp
from jax import lax
from jax.experimental import pallas as pl
from jax.experimental.pallas import tpu as pltpu
from jax.sharding import Mesh
from jax.sharding import PartitionSpec as P


D = 512
H = 8
DH = D // H
REACH = 2
DOM = ("zl", "y", "c")
HEAD = ("zh", "x")
PARTS = (4, 8, 2, 2, 4)
CARRY = DH + 8
TILE_Q = 256
TILE_K = 256
INTERPRET = False


def passed_along(block, axis, distance):
    size = lax.axis_size(axis)
    return lax.ppermute(block, axis, [((i - distance) % size, i) for i in range(size)])


def sent_to_all(block, axis):
    size = lax.axis_size(axis)
    return lax.all_to_all(jnp.broadcast_to(block, (size,) + block.shape), axis, 0, 0)


def matmul(a, b, contract):
    return lax.dot_general(a, b, ((contract[0], contract[1]), ((), ())), preferred_element_type=jnp.float32)


def call(body, outs, scratch=(), smem=(), hbm=(), count=0, flops=0):
    specs = [
        pl.BlockSpec(memory_space=pltpu.SMEM if i in smem else pltpu.HBM if i in hbm else pltpu.VMEM)
        for i in range(count)
    ]
    outputs = [jax.ShapeDtypeStruct(shape, dtype) for shape, dtype in outs]
    return pl.pallas_call(
        body,
        out_shape=outputs if len(outputs) > 1 else outputs[0],
        in_specs=specs,
        out_specs=[pl.BlockSpec(memory_space=pltpu.VMEM) for _ in outs]
        if len(outputs) > 1
        else pl.BlockSpec(memory_space=pltpu.VMEM),
        scratch_shapes=scratch,
        compiler_params=pltpu.CompilerParams(vmem_limit_bytes=48 * 1024 * 1024),
        cost_estimate=pl.CostEstimate(flops=flops, bytes_accessed=2000000, transcendentals=0),
        interpret=INTERPRET,
    )


def project_body(quad, weights, q_out, kv_out, x_out):
    per_z, per_x = quad.shape[1], quad.shape[0]
    for z in range(per_z):
        for x in range(per_x):
            at = (z * per_x + x) * DH
            x_out[at : at + DH, :] = quad[x, z]
    full = x_out[...]
    qkv = matmul(weights[...], full, ((1,), (0,)))
    query = qkv[:DH].astype(jnp.bfloat16).astype(jnp.float32) * (1.0 / math.sqrt(DH))
    for i in range(q_out.shape[0]):
        q_out[i] = query.astype(jnp.bfloat16)
    kv_out[...] = qkv[DH:].astype(jnp.bfloat16)


def three(value):
    high = value.astype(jnp.bfloat16).astype(jnp.float32)
    rest = value - high
    middle = rest.astype(jnp.bfloat16).astype(jnp.float32)
    return [high, middle, rest - middle]


def attend_body(q, kv, x, rows, out, down, up, partner, cross, keys, values, queries, scores_a, scores_b, weights_a, weights_b, results, lists, arrived):
    fetch = pltpu.make_async_copy(rows, lists, arrived)
    fetch.start()
    blocks, _, width = kv.shape
    for j in range(blocks):
        at = slice(j * width, (j + 1) * width)
        keys[at, :] = kv[j, :DH].T
        values[:DH, at] = kv[j, DH:]
    values[DH:, :] = jnp.ones((CARRY - DH, blocks * width), jnp.bfloat16)
    count = q.shape[0]
    for i in range(count):
        queries[:, i * width : (i + 1) * width] = q[i]
    chunks = [slice(j * TILE_K, (j + 1) * TILE_K) for j in range(blocks * width // TILE_K)]
    tiles = count * width // TILE_Q

    def score(asked, scores, chunk, best):
        part = matmul(keys[chunk, :], asked, ((1,), (0,)))
        scores[chunk, :] = part
        high = part.reshape(TILE_K // 8, 8, TILE_Q).max(axis=0)
        return high if best is None else jnp.maximum(best, high)

    def half(tile, scores, scores_next, weights, top):
        following = pl.multiple_of(jnp.minimum(tile + 1, tiles - 1) * TILE_Q, TILE_Q)
        asked = queries[:, pl.ds(following, TILE_Q)]
        best = None
        for chunk in chunks:
            weights[chunk, :] = jnp.exp(scores[chunk, :] - top).astype(jnp.bfloat16)
            best = score(asked, scores_next, chunk, best)
        total = matmul(values[...], weights[...], ((1,), (0,)))
        rows = [total[:DH]] + three(top) + three(total[DH : DH + 1]) + [jnp.zeros((2, TILE_Q), jnp.float32)]
        at = pl.multiple_of(tile * TILE_Q, TILE_Q)
        results[:, pl.ds(at, TILE_Q)] = jnp.concatenate(rows, axis=0).astype(jnp.bfloat16)
        return best.max(axis=0, keepdims=True)

    def step(pair, top):
        top = half(2 * pair, scores_a, scores_b, weights_a, top)
        return half(2 * pair + 1, scores_b, scores_a, weights_b, top)

    best = None
    for chunk in chunks:
        best = score(queries[:, :TILE_Q], scores_a, chunk, best)
    lax.fori_loop(0, tiles // 2, step, best.max(axis=0, keepdims=True))
    for i in range(count):
        out[i] = results[:, i * width : (i + 1) * width]
    fetch.wait()
    core = lax.axis_index("c")
    for j, chosen in ((0, down), (2 * REACH - 1, up), (REACH - core, partner), (REACH - 1 + core, cross)):
        listed = lists[pl.ds(j, 1), :]
        spot = lax.broadcasted_iota(jnp.int32, (x.shape[1], listed.shape[1]), 0) == listed
        chosen[...] = matmul(x[...], spot.astype(jnp.bfloat16), ((1,), (0,))).astype(jnp.bfloat16)


def combine_body(parts, w_out, out):
    count = parts.shape[0]
    tail = [parts[i, DH:, :].astype(jnp.float32) for i in range(count)]
    tops = [t[0:1] + t[1:2] + t[2:3] for t in tail]
    sums = [t[3:4] + t[4:5] + t[5:6] for t in tail]
    best = tops[0]
    for top in tops[1:]:
        best = jnp.maximum(best, top)
    total = jnp.zeros_like(best)
    value = jnp.zeros((DH, best.shape[1]), jnp.float32)
    for i in range(count):
        factor = jnp.exp(tops[i] - best)
        total = total + factor * sums[i]
        value = value + factor * parts[i, :DH, :].astype(jnp.float32)
    heads_out = (value / total).astype(jnp.bfloat16)
    per_x, per_z = out.shape[:2]
    for z in range(per_z):
        for x in range(per_x):
            at = (z * per_x + x) * DH
            share = matmul(w_out[:, at : at + DH], heads_out, ((0,), (0,)))
            out[x, z] = share.astype(jnp.bfloat16)


def fold_body(shares, keep, send):
    mine = lax.axis_index("zh")
    total = [shares[x, mine].astype(jnp.float32) for x in range(shares.shape[0])]
    keep[...] = sum(total[1:], total[0])
    total = [shares[x, 1 - mine].astype(jnp.float32) for x in range(shares.shape[0])]
    send[...] = sum(total[1:], total[0]).astype(jnp.bfloat16)


def message_body(x, down, up, partner, cross, tiles, counts, cols, w_msg, own_x, out, table):
    own, slots, size, _ = tiles.shape
    for b in range(own):
        table[b] = x[:, b * size : (b + 1) * size]
    core = lax.axis_index("c")
    for j, received in ((0, down), (2 * REACH - 1, up), (REACH - 1 + core, partner), (REACH - core, cross)):
        table[own + j] = received[...]
    for r in range(own):
        total = jnp.zeros((D, size), jnp.float32)
        for t in range(slots):
            tile = tiles[r, t]
            tile = jnp.where(t < counts[r], tile, jnp.zeros_like(tile))
            total = total + matmul(table[cols[r, t]], tile, ((1,), (1,)))
        projected = matmul(w_msg[...], total.astype(jnp.bfloat16), ((1,), (0,)))
        at = slice(r * size, (r + 1) * size)
        out[:, at] = own_x[:, at].astype(jnp.float32) + jnp.maximum(projected, 0.0)


def local(node_feats, tile_vals, tile_counts, tile_cols, send_rows, w_msg, w_qkv, w_out):
    rows = node_feats.shape[0]
    bf16, f32 = jnp.bfloat16, jnp.float32
    listed = send_rows[0]
    directions, bound = listed.shape
    askers, givers = lax.axis_size("y"), lax.axis_size(("zl", "c"))
    keys, asked = givers * rows, askers * rows
    x_own = node_feats.T
    pair = lax.all_gather(x_own, "zh", axis=0, tiled=False)
    quad = sent_to_all(pair, "x")
    weights = jnp.swapaxes(w_qkv, 1, 2).reshape(3 * DH, D)
    q, kv, x_full = call(
        project_body,
        [((askers, DH, rows), bf16), ((2 * DH, rows), bf16), ((D, rows), bf16)],
        count=2,
        flops=2 * D * rows * 3 * DH,
    )(quad, weights)
    queries = lax.all_to_all(q, "y", 0, 0)
    held = lax.all_gather(kv, ("zl", "c"), axis=0, tiled=False)
    parts, down, up, partner, cross = call(
        attend_body,
        [((askers, CARRY, rows), bf16)] + [((D, bound), bf16)] * directions,
        scratch=[
            pltpu.VMEM((keys, DH), bf16),
            pltpu.VMEM((CARRY, keys), bf16),
            pltpu.VMEM((DH, asked), bf16),
            pltpu.VMEM((keys, TILE_Q), f32),
            pltpu.VMEM((keys, TILE_Q), f32),
            pltpu.VMEM((keys, TILE_Q), bf16),
            pltpu.VMEM((keys, TILE_Q), bf16),
            pltpu.VMEM((CARRY, asked), bf16),
            pltpu.VMEM((directions, bound), jnp.int32),
            pltpu.SemaphoreType.DMA,
        ],
        hbm=(3,),
        count=4,
        flops=4 * DH * keys * asked,
    )(queries, held, x_full, pltpu.with_memory_space_constraint(listed, pltpu.HBM))
    parts = lax.all_to_all(parts, "y", 0, 0)
    per_x, per_z = lax.axis_size("x"), lax.axis_size("zh")
    shares = call(
        combine_body, [((per_x, per_z, DH, rows), bf16)], count=2, flops=2 * D * DH * rows
    )(parts, w_out)
    down = passed_along(down, DOM, -REACH)
    up = passed_along(up, DOM, REACH)
    size = lax.axis_size(DOM)
    cross = lax.ppermute(cross, DOM, [(i, (i + (1 if i % 2 else -1)) % size) for i in range(size)])
    partner = passed_along(partner, "c", 1)
    shares = lax.all_to_all(shares, "x", 0, 0)
    base = call(
        message_body,
        [((DH, rows), f32)],
        scratch=[pltpu.VMEM((rows // bound + directions, D, bound), bf16)],
        smem=(6, 7),
        count=10,
        flops=2 * D * rows * (4 * bound + DH),
    )(x_full, down, up, partner, cross, tile_vals, tile_counts, tile_cols, w_msg.T, x_own)
    keep, send = call(
        fold_body, [((DH, rows), f32), ((DH, rows), bf16)], count=1, flops=D * rows
    )(shares)
    halves = lax.all_gather(send, "zh", axis=0, tiled=False)
    others = jnp.where(lax.axis_index("zh") == 0, halves[1], halves[0])
    return (base + keep + others.astype(f32)).astype(bf16).T


def solution(mesh):
    parts = Mesh(mesh.devices.reshape(PARTS), DOM + HEAD)
    placed = (
        P(DOM, HEAD),
        P(DOM, None, None, None),
        P(DOM),
        P(DOM, None),
        P(DOM, None, None),
        P(None, HEAD),
        P(None, None, HEAD),
        P(HEAD, None),
    )
    return jax.shard_map(local, mesh=parts, in_specs=placed, out_specs=P(DOM, HEAD), check_vma=False)
```

```python
import math

import jax
import jax.numpy as jnp
from jax import lax
from jax.experimental import pallas as pl
from jax.experimental.pallas import tpu as pltpu
from jax.sharding import Mesh
from jax.sharding import PartitionSpec as P


D = 512
H = 8
DH = D // H
REACH = 2
DOM = ("zl", "y", "c")
HEAD = ("zh", "x")
PARTS = (4, 8, 2, 2, 4)
CARRY = DH + 8
TILE_Q = 256
TILE_K = 256
INTERPRET = False


def offsets(reach_count):
    return [
        position - reach_count if position < reach_count else position - reach_count + 1
        for position in range(2 * reach_count)
    ]


def passed_along(block, axis, distance):
    size = lax.axis_size(axis)
    return lax.ppermute(block, axis, [((i - distance) % size, i) for i in range(size)])


def sent_to_all(block, axis):
    size = lax.axis_size(axis)
    return lax.all_to_all(jnp.broadcast_to(block, (size,) + block.shape), axis, 0, 0)


def matmul(a, b, contract):
    return lax.dot_general(a, b, ((contract[0], contract[1]), ((), ())), preferred_element_type=jnp.float32)


def call(body, outs, scratch=(), smem=(), hbm=(), count=0, flops=0):
    specs = [
        pl.BlockSpec(memory_space=pltpu.SMEM if i in smem else pltpu.HBM if i in hbm else pltpu.VMEM)
        for i in range(count)
    ]
    outputs = [jax.ShapeDtypeStruct(shape, dtype) for shape, dtype in outs]
    return pl.pallas_call(
        body,
        out_shape=outputs if len(outputs) > 1 else outputs[0],
        in_specs=specs,
        out_specs=[pl.BlockSpec(memory_space=pltpu.VMEM) for _ in outs]
        if len(outputs) > 1
        else pl.BlockSpec(memory_space=pltpu.VMEM),
        scratch_shapes=scratch,
        compiler_params=pltpu.CompilerParams(vmem_limit_bytes=48 * 1024 * 1024),
        cost_estimate=pl.CostEstimate(flops=flops, bytes_accessed=2000000, transcendentals=0),
        interpret=INTERPRET,
    )


def project_body(quad, weights, q_out, kv_out, x_out):
    per_z, per_x = quad.shape[1], quad.shape[0]
    for z in range(per_z):
        for x in range(per_x):
            at = (z * per_x + x) * DH
            x_out[at : at + DH, :] = quad[x, z]
    full = x_out[...]
    qkv = matmul(weights[...], full, ((1,), (0,)))
    query = qkv[:DH].astype(jnp.bfloat16).astype(jnp.float32) * (1.0 / math.sqrt(DH))
    for i in range(q_out.shape[0]):
        q_out[i] = query.astype(jnp.bfloat16)
    kv_out[...] = qkv[DH:].astype(jnp.bfloat16)


def three(value):
    high = value.astype(jnp.bfloat16).astype(jnp.float32)
    rest = value - high
    middle = rest.astype(jnp.bfloat16).astype(jnp.float32)
    return [high, middle, rest - middle]


def attend_body(q, kv, x, rows, out, *rest):
    *chosen, keys, values, queries, scores_a, scores_b, weights_a, weights_b, results, lists, arrived = rest
    fetch = pltpu.make_async_copy(rows, lists, arrived)
    fetch.start()
    blocks, _, width = kv.shape
    for j in range(blocks):
        at = slice(j * width, (j + 1) * width)
        keys[at, :] = kv[j, :DH].T
        values[:DH, at] = kv[j, DH:]
    values[DH:, :] = jnp.ones((CARRY - DH, blocks * width), jnp.bfloat16)
    count = q.shape[0]
    for i in range(count):
        queries[:, i * width : (i + 1) * width] = q[i]
    chunks = [slice(j * TILE_K, (j + 1) * TILE_K) for j in range(blocks * width // TILE_K)]
    tiles = count * width // TILE_Q

    def score(asked, scores, chunk, best):
        part = matmul(keys[chunk, :], asked, ((1,), (0,)))
        scores[chunk, :] = part
        high = part.reshape(TILE_K // 8, 8, TILE_Q).max(axis=0)
        return high if best is None else jnp.maximum(best, high)

    def half(tile, scores, scores_next, weights, top):
        following = pl.multiple_of(jnp.minimum(tile + 1, tiles - 1) * TILE_Q, TILE_Q)
        asked = queries[:, pl.ds(following, TILE_Q)]
        best = None
        for chunk in chunks:
            weights[chunk, :] = jnp.exp(scores[chunk, :] - top).astype(jnp.bfloat16)
            best = score(asked, scores_next, chunk, best)
        total = matmul(values[...], weights[...], ((1,), (0,)))
        rows = [total[:DH]] + three(top) + three(total[DH : DH + 1]) + [jnp.zeros((2, TILE_Q), jnp.float32)]
        at = pl.multiple_of(tile * TILE_Q, TILE_Q)
        results[:, pl.ds(at, TILE_Q)] = jnp.concatenate(rows, axis=0).astype(jnp.bfloat16)
        return best.max(axis=0, keepdims=True)

    def step(pair, top):
        top = half(2 * pair, scores_a, scores_b, weights_a, top)
        return half(2 * pair + 1, scores_b, scores_a, weights_b, top)

    best = None
    for chunk in chunks:
        best = score(queries[:, :TILE_Q], scores_a, chunk, best)
    lax.fori_loop(0, tiles // 2, step, best.max(axis=0, keepdims=True))
    for i in range(count):
        out[i] = results[:, i * width : (i + 1) * width]
    fetch.wait()
    for j, block in enumerate(chosen):
        listed = lists[j : j + 1, :]
        spot = lax.broadcasted_iota(jnp.int32, (x.shape[1], listed.shape[1]), 0) == listed
        block[...] = matmul(x[...], spot.astype(jnp.bfloat16), ((1,), (0,))).astype(jnp.bfloat16)


def combine_body(parts, w_out, out):
    count = parts.shape[0]
    tail = [parts[i, DH:, :].astype(jnp.float32) for i in range(count)]
    tops = [t[0:1] + t[1:2] + t[2:3] for t in tail]
    sums = [t[3:4] + t[4:5] + t[5:6] for t in tail]
    best = tops[0]
    for top in tops[1:]:
        best = jnp.maximum(best, top)
    total = jnp.zeros_like(best)
    value = jnp.zeros((DH, best.shape[1]), jnp.float32)
    for i in range(count):
        factor = jnp.exp(tops[i] - best)
        total = total + factor * sums[i]
        value = value + factor * parts[i, :DH, :].astype(jnp.float32)
    heads_out = (value / total).astype(jnp.bfloat16)
    per_x, per_z = out.shape[:2]
    for z in range(per_z):
        for x in range(per_x):
            at = (z * per_x + x) * DH
            share = matmul(w_out[:, at : at + DH], heads_out, ((0,), (0,)))
            out[x, z] = share.astype(jnp.bfloat16)


def fold_body(shares, keep, send):
    mine = lax.axis_index("zh")
    total = [shares[x, mine].astype(jnp.float32) for x in range(shares.shape[0])]
    keep[...] = sum(total[1:], total[0])
    total = [shares[x, 1 - mine].astype(jnp.float32) for x in range(shares.shape[0])]
    send[...] = sum(total[1:], total[0]).astype(jnp.bfloat16)


def message_body(x, r0, r1, r2, r3, tiles, counts, cols, w_msg, own_x, out, table):
    own, slots, size, _ = tiles.shape
    for b in range(own):
        table[b] = x[:, b * size : (b + 1) * size]
    for j, received in enumerate((r0, r1, r2, r3)):
        table[own + j] = received[...]
    for r in range(own):
        total = jnp.zeros((D, size), jnp.float32)
        for t in range(slots):
            tile = tiles[r, t]
            tile = jnp.where(t < counts[r], tile, jnp.zeros_like(tile))
            total = total + matmul(table[cols[r, t]], tile, ((1,), (1,)))
        projected = matmul(w_msg[...], total.astype(jnp.bfloat16), ((1,), (0,)))
        at = slice(r * size, (r + 1) * size)
        out[:, at] = own_x[:, at].astype(jnp.float32) + jnp.maximum(projected, 0.0)


def local(node_feats, tile_vals, tile_counts, tile_cols, send_rows, w_msg, w_qkv, w_out):
    rows = node_feats.shape[0]
    bf16, f32 = jnp.bfloat16, jnp.float32
    listed = send_rows[0]
    directions, bound = listed.shape
    askers, givers = lax.axis_size("y"), lax.axis_size(("zl", "c"))
    keys, asked = givers * rows, askers * rows
    x_own = node_feats.T
    pair = lax.all_gather(x_own, "zh", axis=0, tiled=False)
    quad = sent_to_all(pair, "x")
    weights = jnp.swapaxes(w_qkv, 1, 2).reshape(3 * DH, D)
    q, kv, x_full = call(
        project_body,
        [((askers, DH, rows), bf16), ((2 * DH, rows), bf16), ((D, rows), bf16)],
        count=2,
        flops=2 * D * rows * 3 * DH,
    )(quad, weights)
    queries = lax.all_to_all(q, "y", 0, 0)
    held = lax.all_gather(kv, ("zl", "c"), axis=0, tiled=False)
    parts, *chosen = call(
        attend_body,
        [((askers, CARRY, rows), bf16)] + [((D, bound), bf16)] * directions,
        scratch=[
            pltpu.VMEM((keys, DH), bf16),
            pltpu.VMEM((CARRY, keys), bf16),
            pltpu.VMEM((DH, asked), bf16),
            pltpu.VMEM((keys, TILE_Q), f32),
            pltpu.VMEM((keys, TILE_Q), f32),
            pltpu.VMEM((keys, TILE_Q), bf16),
            pltpu.VMEM((keys, TILE_Q), bf16),
            pltpu.VMEM((CARRY, asked), bf16),
            pltpu.VMEM((directions, bound), jnp.int32),
            pltpu.SemaphoreType.DMA,
        ],
        hbm=(3,),
        count=4,
        flops=4 * DH * keys * asked,
    )(queries, held, x_full, pltpu.with_memory_space_constraint(listed, pltpu.HBM))
    parts = lax.all_to_all(parts, "y", 0, 0)
    per_x, per_z = lax.axis_size("x"), lax.axis_size("zh")
    shares = call(
        combine_body, [((per_x, per_z, DH, rows), bf16)], count=2, flops=2 * D * DH * rows
    )(parts, w_out)
    received = []
    for block, offset in zip(chosen, offsets(REACH)):
        received.append(passed_along(block, DOM, offset))
    shares = lax.all_to_all(shares, "x", 0, 0)
    base = call(
        message_body,
        [((DH, rows), f32)],
        scratch=[pltpu.VMEM((rows // bound + directions, D, bound), bf16)],
        smem=(6, 7),
        count=10,
        flops=2 * D * rows * (4 * bound + DH),
    )(x_full, *received, tile_vals, tile_counts, tile_cols, w_msg.T, x_own)
    keep, send = call(
        fold_body, [((DH, rows), f32), ((DH, rows), bf16)], count=1, flops=D * rows
    )(shares)
    halves = lax.all_gather(send, "zh", axis=0, tiled=False)
    others = jnp.where(lax.axis_index("zh") == 0, halves[1], halves[0])
    return (base + keep + others.astype(f32)).astype(bf16).T


def solution(mesh):
    parts = Mesh(mesh.devices.reshape(PARTS), DOM + HEAD)
    placed = (
        P(DOM, HEAD),
        P(DOM, None, None, None),
        P(DOM),
        P(DOM, None),
        P(DOM, None, None),
        P(None, HEAD),
        P(None, None, HEAD),
        P(HEAD, None),
    )
    return jax.shard_map(local, mesh=parts, in_specs=placed, out_specs=P(DOM, HEAD), check_vma=False)
```

```python
import math

import jax
import jax.numpy as jnp
from jax import lax
from jax.experimental import pallas as pl
from jax.experimental.pallas import tpu as pltpu
from jax.sharding import Mesh
from jax.sharding import PartitionSpec as P


D = 512
H = 8
DH = D // H
REACH = 2
DOM = ("zl", "y", "c")
HEAD = ("zh", "x")
PARTS = (4, 8, 2, 2, 4)
CARRY = DH + 8
TILE_Q = 256
TILE_K = 256
INTERPRET = False


def offsets(reach_count):
    return [
        position - reach_count if position < reach_count else position - reach_count + 1
        for position in range(2 * reach_count)
    ]


def passed_along(block, axis, distance):
    size = lax.axis_size(axis)
    return lax.ppermute(block, axis, [((i - distance) % size, i) for i in range(size)])


def sent_to_all(block, axis):
    size = lax.axis_size(axis)
    return lax.all_to_all(jnp.broadcast_to(block, (size,) + block.shape), axis, 0, 0)


def matmul(a, b, contract):
    return lax.dot_general(a, b, ((contract[0], contract[1]), ((), ())), preferred_element_type=jnp.float32)


def call(body, outs, scratch=(), smem=(), hbm=(), count=0, flops=0):
    specs = [
        pl.BlockSpec(memory_space=pltpu.SMEM if i in smem else pltpu.HBM if i in hbm else pltpu.VMEM)
        for i in range(count)
    ]
    outputs = [jax.ShapeDtypeStruct(shape, dtype) for shape, dtype in outs]
    return pl.pallas_call(
        body,
        out_shape=outputs if len(outputs) > 1 else outputs[0],
        in_specs=specs,
        out_specs=[pl.BlockSpec(memory_space=pltpu.VMEM) for _ in outs]
        if len(outputs) > 1
        else pl.BlockSpec(memory_space=pltpu.VMEM),
        scratch_shapes=scratch,
        compiler_params=pltpu.CompilerParams(vmem_limit_bytes=48 * 1024 * 1024),
        cost_estimate=pl.CostEstimate(flops=flops, bytes_accessed=2000000, transcendentals=0),
        interpret=INTERPRET,
    )


def project_body(quad, weights, q_out, kv_out, x_out):
    per_z, per_x = quad.shape[1], quad.shape[0]
    for z in range(per_z):
        for x in range(per_x):
            at = (z * per_x + x) * DH
            x_out[at : at + DH, :] = quad[x, z]
    full = x_out[...]
    qkv = matmul(weights[...], full, ((1,), (0,)))
    query = qkv[:DH].astype(jnp.bfloat16).astype(jnp.float32) * (1.0 / math.sqrt(DH))
    for i in range(q_out.shape[0]):
        q_out[i] = query.astype(jnp.bfloat16)
    kv_out[...] = qkv[DH:].astype(jnp.bfloat16)


def three(value):
    high = value.astype(jnp.bfloat16).astype(jnp.float32)
    rest = value - high
    middle = rest.astype(jnp.bfloat16).astype(jnp.float32)
    return [high, middle, rest - middle]


def attend_body(q, kv, x, rows, out, *rest):
    *chosen, keys, values, queries, scores_a, scores_b, weights_a, weights_b, results, lists, arrived = rest
    fetch = pltpu.make_async_copy(rows, lists, arrived)
    fetch.start()
    blocks, _, width = kv.shape
    for j in range(blocks):
        at = slice(j * width, (j + 1) * width)
        keys[at, :] = kv[j, :DH].T
        values[:DH, at] = kv[j, DH:]
    values[DH:, :] = jnp.ones((CARRY - DH, blocks * width), jnp.bfloat16)
    count = q.shape[0]
    for i in range(count):
        queries[:, i * width : (i + 1) * width] = q[i]
    chunks = [slice(j * TILE_K, (j + 1) * TILE_K) for j in range(blocks * width // TILE_K)]
    tiles = count * width // TILE_Q

    def score(asked, scores, chunk, best):
        part = matmul(keys[chunk, :], asked, ((1,), (0,)))
        scores[chunk, :] = part
        high = part.reshape(TILE_K // 8, 8, TILE_Q).max(axis=0)
        return high if best is None else jnp.maximum(best, high)

    def half(tile, scores, scores_next, weights, top):
        following = pl.multiple_of(jnp.minimum(tile + 1, tiles - 1) * TILE_Q, TILE_Q)
        asked = queries[:, pl.ds(following, TILE_Q)]
        best = None
        for chunk in chunks:
            weights[chunk, :] = jnp.exp(scores[chunk, :] - top).astype(jnp.bfloat16)
            best = score(asked, scores_next, chunk, best)
        total = matmul(values[...], weights[...], ((1,), (0,)))
        rows = [total[:DH]] + three(top) + three(total[DH : DH + 1]) + [jnp.zeros((2, TILE_Q), jnp.float32)]
        at = pl.multiple_of(tile * TILE_Q, TILE_Q)
        results[:, pl.ds(at, TILE_Q)] = jnp.concatenate(rows, axis=0).astype(jnp.bfloat16)
        return best.max(axis=0, keepdims=True)

    def step(pair, top):
        top = half(2 * pair, scores_a, scores_b, weights_a, top)
        return half(2 * pair + 1, scores_b, scores_a, weights_b, top)

    best = None
    for chunk in chunks:
        best = score(queries[:, :TILE_Q], scores_a, chunk, best)
    lax.fori_loop(0, tiles // 2, step, best.max(axis=0, keepdims=True))
    for i in range(count):
        out[i] = results[:, i * width : (i + 1) * width]
    fetch.wait()
    for j, block in enumerate(chosen):
        listed = lists[j : j + 1, :]
        spot = lax.broadcasted_iota(jnp.int32, (x.shape[1], listed.shape[1]), 0) == listed
        block[...] = matmul(x[...], spot.astype(jnp.bfloat16), ((1,), (0,))).astype(jnp.bfloat16)


def combine_body(parts, w_out, other, own, shares):
    count = parts.shape[0]
    tail = [parts[i, DH:, :].astype(jnp.float32) for i in range(count)]
    tops = [t[0:1] + t[1:2] + t[2:3] for t in tail]
    sums = [t[3:4] + t[4:5] + t[5:6] for t in tail]
    best = tops[0]
    for top in tops[1:]:
        best = jnp.maximum(best, top)
    total = jnp.zeros_like(best)
    value = jnp.zeros((DH, best.shape[1]), jnp.float32)
    for i in range(count):
        factor = jnp.exp(tops[i] - best)
        total = total + factor * sums[i]
        value = value + factor * parts[i, :DH, :].astype(jnp.float32)
    heads_out = (value / total).astype(jnp.bfloat16)
    per_z, per_x = shares.shape[:2]
    for z in range(per_z):
        for x in range(per_x):
            at = (z * per_x + x) * DH
            share = matmul(w_out[:, at : at + DH], heads_out, ((0,), (0,)))
            shares[z, x] = share.astype(jnp.bfloat16)
    mine = lax.axis_index("zh")
    other[...] = shares[1 - mine]
    own[...] = shares[mine]


def fold_body(shares, out):
    total = [shares[x].astype(jnp.float32) for x in range(shares.shape[0])]
    out[...] = sum(total[1:], total[0]).astype(out.dtype)


def message_body(x, r0, r1, r2, r3, tiles, counts, cols, w_msg, own_x, out, table):
    own, slots, size, _ = tiles.shape
    for b in range(own):
        table[b] = x[:, b * size : (b + 1) * size]
    for j, received in enumerate((r0, r1, r2, r3)):
        table[own + j] = received[...]
    for r in range(own):
        total = jnp.zeros((D, size), jnp.float32)
        for t in range(slots):
            tile = tiles[r, t]
            tile = jnp.where(t < counts[r], tile, jnp.zeros_like(tile))
            total = total + matmul(table[cols[r, t]], tile, ((1,), (1,)))
        projected = matmul(w_msg[...], total.astype(jnp.bfloat16), ((1,), (0,)))
        at = slice(r * size, (r + 1) * size)
        out[:, at] = own_x[:, at].astype(jnp.float32) + jnp.maximum(projected, 0.0)


def local(node_feats, tile_vals, tile_counts, tile_cols, send_rows, w_msg, w_qkv, w_out):
    rows = node_feats.shape[0]
    bf16, f32 = jnp.bfloat16, jnp.float32
    listed = send_rows[0]
    directions, bound = listed.shape
    askers, givers = lax.axis_size("y"), lax.axis_size(("zl", "c"))
    keys, asked = givers * rows, askers * rows
    x_own = node_feats.T
    pair = lax.all_gather(x_own, "zh", axis=0, tiled=False)
    quad = sent_to_all(pair, "x")
    weights = jnp.swapaxes(w_qkv, 1, 2).reshape(3 * DH, D)
    q, kv, x_full = call(
        project_body,
        [((askers, DH, rows), bf16), ((2 * DH, rows), bf16), ((D, rows), bf16)],
        count=2,
        flops=2 * D * rows * 3 * DH,
    )(quad, weights)
    queries = lax.all_to_all(q, "y", 0, 0)
    held = lax.all_gather(kv, ("zl", "c"), axis=0, tiled=False)
    parts, *chosen = call(
        attend_body,
        [((askers, CARRY, rows), bf16)] + [((D, bound), bf16)] * directions,
        scratch=[
            pltpu.VMEM((keys, DH), bf16),
            pltpu.VMEM((CARRY, keys), bf16),
            pltpu.VMEM((DH, asked), bf16),
            pltpu.VMEM((keys, TILE_Q), f32),
            pltpu.VMEM((keys, TILE_Q), f32),
            pltpu.VMEM((keys, TILE_Q), bf16),
            pltpu.VMEM((keys, TILE_Q), bf16),
            pltpu.VMEM((CARRY, asked), bf16),
            pltpu.VMEM((directions, bound), jnp.int32),
            pltpu.SemaphoreType.DMA,
        ],
        hbm=(3,),
        count=4,
        flops=4 * DH * keys * asked,
    )(queries, held, x_full, pltpu.with_memory_space_constraint(listed, pltpu.HBM))
    parts = lax.all_to_all(parts, "y", 0, 0)
    per_x, per_z = lax.axis_size("x"), lax.axis_size("zh")
    other, own = call(
        combine_body,
        [((per_x, DH, rows), bf16)] * per_z,
        scratch=[pltpu.VMEM((per_z, per_x, DH, rows), bf16)],
        count=2,
        flops=2 * D * DH * rows,
    )(parts, w_out)
    received = [passed_along(block, DOM, o) for block, o in zip(chosen, offsets(REACH))]
    other = lax.all_to_all(other, "x", 0, 0)
    base = call(
        message_body,
        [((DH, rows), f32)],
        scratch=[pltpu.VMEM((rows // bound + directions, D, bound), bf16)],
        smem=(6, 7),
        count=10,
        flops=2 * D * rows * (4 * bound + DH),
    )(x_full, *received, tile_vals, tile_counts, tile_cols, w_msg.T, x_own)
    send = call(fold_body, [((DH, rows), bf16)], count=1, flops=D * rows)(other)
    own = lax.all_to_all(own, "x", 0, 0)
    halves = lax.all_gather(send, "zh", axis=0, tiled=False)
    keep = own.astype(f32).sum(axis=0)
    others = jnp.where(lax.axis_index("zh") == 0, halves[1], halves[0])
    return (base + keep + others.astype(f32)).astype(bf16).T


def solution(mesh):
    parts = Mesh(mesh.devices.reshape(PARTS), DOM + HEAD)
    placed = (
        P(DOM, HEAD),
        P(DOM, None, None, None),
        P(DOM),
        P(DOM, None),
        P(DOM, None, None),
        P(None, HEAD),
        P(None, None, HEAD),
        P(HEAD, None),
    )
    return jax.shard_map(local, mesh=parts, in_specs=placed, out_specs=P(DOM, HEAD), check_vma=False)
```

```python
import math

import jax
import jax.numpy as jnp
from jax import lax
from jax.experimental import pallas as pl
from jax.experimental.pallas import tpu as pltpu
from jax.sharding import Mesh
from jax.sharding import PartitionSpec as P


D = 512
H = 8
DH = D // H
REACH = 2
DOM = ("zl", "y", "c")
HEAD = ("zh", "x")
PARTS = (4, 8, 2, 2, 4)
CARRY = DH + 8
TILE_Q = 256
TILE_K = 256
RING = [0, 2, 4, 6, 7, 5, 3, 1]
INTERPRET = False


def offsets(reach_count):
    return [
        position - reach_count if position < reach_count else position - reach_count + 1
        for position in range(2 * reach_count)
    ]


def passed_along(block, axis, distance):
    size = lax.axis_size(axis)
    return lax.ppermute(block, axis, [((i - distance) % size, i) for i in range(size)])


def sent_to_all(block, axis):
    size = lax.axis_size(axis)
    return lax.all_to_all(jnp.broadcast_to(block, (size,) + block.shape), axis, 0, 0)


def matmul(a, b, contract):
    return lax.dot_general(a, b, ((contract[0], contract[1]), ((), ())), preferred_element_type=jnp.float32)


def call(body, outs, scratch=(), smem=(), hbm=(), count=0, flops=0):
    specs = [
        pl.BlockSpec(memory_space=pltpu.SMEM if i in smem else pltpu.HBM if i in hbm else pltpu.VMEM)
        for i in range(count)
    ]
    outputs = [jax.ShapeDtypeStruct(shape, dtype) for shape, dtype in outs]
    return pl.pallas_call(
        body,
        out_shape=outputs if len(outputs) > 1 else outputs[0],
        in_specs=specs,
        out_specs=[pl.BlockSpec(memory_space=pltpu.VMEM) for _ in outs]
        if len(outputs) > 1
        else pl.BlockSpec(memory_space=pltpu.VMEM),
        scratch_shapes=scratch,
        compiler_params=pltpu.CompilerParams(vmem_limit_bytes=48 * 1024 * 1024),
        cost_estimate=pl.CostEstimate(flops=flops, bytes_accessed=2000000, transcendentals=0),
        interpret=INTERPRET,
    )


def project_body(quad, weights, q_out, kv_out, x_out):
    per_z, per_x = quad.shape[1], quad.shape[0]
    for z in range(per_z):
        for x in range(per_x):
            at = (z * per_x + x) * DH
            x_out[at : at + DH, :] = quad[x, z]
    full = x_out[...]
    qkv = matmul(weights[...], full, ((1,), (0,)))
    query = qkv[:DH].astype(jnp.bfloat16).astype(jnp.float32) * (1.0 / math.sqrt(DH))
    for i in range(q_out.shape[0]):
        q_out[i] = query.astype(jnp.bfloat16)
    kv_out[...] = qkv[DH:].astype(jnp.bfloat16)


def three(value):
    high = value.astype(jnp.bfloat16).astype(jnp.float32)
    rest = value - high
    middle = rest.astype(jnp.bfloat16).astype(jnp.float32)
    return [high, middle, rest - middle]


def attend_body(q, kv, x, rows, out, *rest):
    *chosen, keys, values, queries, scores_a, scores_b, weights_a, weights_b, results, lists, arrived = rest
    fetch = pltpu.make_async_copy(rows, lists, arrived)
    fetch.start()
    blocks, _, width = kv.shape
    for j in range(blocks):
        at = slice(j * width, (j + 1) * width)
        keys[at, :] = kv[j, :DH].T
        values[:DH, at] = kv[j, DH:]
    values[DH:, :] = jnp.ones((CARRY - DH, blocks * width), jnp.bfloat16)
    count = q.shape[0]
    for i in range(count):
        queries[:, i * width : (i + 1) * width] = q[i]
    chunks = [slice(j * TILE_K, (j + 1) * TILE_K) for j in range(blocks * width // TILE_K)]
    tiles = count * width // TILE_Q

    def score(asked, scores, chunk, best):
        part = matmul(keys[chunk, :], asked, ((1,), (0,)))
        scores[chunk, :] = part
        high = part.reshape(TILE_K // 8, 8, TILE_Q).max(axis=0)
        return high if best is None else jnp.maximum(best, high)

    def half(tile, scores, scores_next, weights, top):
        following = pl.multiple_of(jnp.minimum(tile + 1, tiles - 1) * TILE_Q, TILE_Q)
        asked = queries[:, pl.ds(following, TILE_Q)]
        best = None
        for chunk in chunks:
            weights[chunk, :] = jnp.exp(scores[chunk, :] - top).astype(jnp.bfloat16)
            best = score(asked, scores_next, chunk, best)
        total = matmul(values[...], weights[...], ((1,), (0,)))
        rows = [total[:DH]] + three(top) + three(total[DH : DH + 1]) + [jnp.zeros((2, TILE_Q), jnp.float32)]
        at = pl.multiple_of(tile * TILE_Q, TILE_Q)
        results[:, pl.ds(at, TILE_Q)] = jnp.concatenate(rows, axis=0).astype(jnp.bfloat16)
        return best.max(axis=0, keepdims=True)

    def step(pair, top):
        top = half(2 * pair, scores_a, scores_b, weights_a, top)
        return half(2 * pair + 1, scores_b, scores_a, weights_b, top)

    best = None
    for chunk in chunks:
        best = score(queries[:, :TILE_Q], scores_a, chunk, best)
    lax.fori_loop(0, tiles // 2, step, best.max(axis=0, keepdims=True))
    for i in range(count):
        out[i] = results[:, i * width : (i + 1) * width]
    fetch.wait()
    for j, block in enumerate(chosen):
        listed = lists[j : j + 1, :]
        spot = lax.broadcasted_iota(jnp.int32, (x.shape[1], listed.shape[1]), 0) == listed
        block[...] = matmul(x[...], spot.astype(jnp.bfloat16), ((1,), (0,))).astype(jnp.bfloat16)


def combine_body(parts, w_out, out):
    count = parts.shape[0]
    tail = [parts[i, DH:, :].astype(jnp.float32) for i in range(count)]
    tops = [t[0:1] + t[1:2] + t[2:3] for t in tail]
    sums = [t[3:4] + t[4:5] + t[5:6] for t in tail]
    best = tops[0]
    for top in tops[1:]:
        best = jnp.maximum(best, top)
    total = jnp.zeros_like(best)
    value = jnp.zeros((DH, best.shape[1]), jnp.float32)
    for i in range(count):
        factor = jnp.exp(tops[i] - best)
        total = total + factor * sums[i]
        value = value + factor * parts[i, :DH, :].astype(jnp.float32)
    heads_out = (value / total).astype(jnp.bfloat16)
    per_x, per_z = out.shape[:2]
    for z in range(per_z):
        for x in range(per_x):
            at = (z * per_x + x) * DH
            share = matmul(w_out[:, at : at + DH], heads_out, ((0,), (0,)))
            out[x, z] = share.astype(jnp.bfloat16)


def fold_body(shares, keep, send):
    mine = lax.axis_index("zh")
    total = [shares[x, mine].astype(jnp.float32) for x in range(shares.shape[0])]
    keep[...] = sum(total[1:], total[0])
    total = [shares[x, 1 - mine].astype(jnp.float32) for x in range(shares.shape[0])]
    send[...] = sum(total[1:], total[0]).astype(jnp.bfloat16)


def message_body(x, r0, r1, r2, r3, tiles, counts, cols, w_msg, own_x, out, table):
    own, slots, size, _ = tiles.shape
    for b in range(own):
        table[b] = x[:, b * size : (b + 1) * size]
    for j, received in enumerate((r0, r1, r2, r3)):
        table[own + j] = received[...]
    for r in range(own):
        total = jnp.zeros((D, size), jnp.float32)
        for t in range(slots):
            tile = tiles[r, t]
            tile = jnp.where(t < counts[r], tile, jnp.zeros_like(tile))
            total = total + matmul(table[cols[r, t]], tile, ((1,), (1,)))
        projected = matmul(w_msg[...], total.astype(jnp.bfloat16), ((1,), (0,)))
        at = slice(r * size, (r + 1) * size)
        out[:, at] = own_x[:, at].astype(jnp.float32) + jnp.maximum(projected, 0.0)


def local(node_feats, tile_vals, tile_counts, tile_cols, send_rows, w_msg, w_qkv, w_out):
    rows = node_feats.shape[0]
    bf16, f32 = jnp.bfloat16, jnp.float32
    listed = send_rows[0]
    directions, bound = listed.shape
    askers, givers = lax.axis_size("y"), lax.axis_size(("zl", "c"))
    keys, asked = givers * rows, askers * rows
    x_own = node_feats.T
    pair = lax.all_gather(x_own, "zh", axis=0, tiled=False)
    quad = sent_to_all(pair, "x")
    weights = jnp.swapaxes(w_qkv, 1, 2).reshape(3 * DH, D)
    q, kv, x_full = call(
        project_body,
        [((askers, DH, rows), bf16), ((2 * DH, rows), bf16), ((D, rows), bf16)],
        count=2,
        flops=2 * D * rows * 3 * DH,
    )(quad, weights)
    queries = lax.all_to_all(q, "y", 0, 0)
    held = lax.all_gather(kv, ("zl", "c"), axis=0, tiled=False, axis_index_groups=[RING])
    parts, *chosen = call(
        attend_body,
        [((askers, CARRY, rows), bf16)] + [((D, bound), bf16)] * directions,
        scratch=[
            pltpu.VMEM((keys, DH), bf16),
            pltpu.VMEM((CARRY, keys), bf16),
            pltpu.VMEM((DH, asked), bf16),
            pltpu.VMEM((keys, TILE_Q), f32),
            pltpu.VMEM((keys, TILE_Q), f32),
            pltpu.VMEM((keys, TILE_Q), bf16),
            pltpu.VMEM((keys, TILE_Q), bf16),
            pltpu.VMEM((CARRY, asked), bf16),
            pltpu.VMEM((directions, bound), jnp.int32),
            pltpu.SemaphoreType.DMA,
        ],
        hbm=(3,),
        count=4,
        flops=4 * DH * keys * asked,
    )(queries, held, x_full, pltpu.with_memory_space_constraint(listed, pltpu.HBM))
    parts = lax.all_to_all(parts, "y", 0, 0)
    per_x, per_z = lax.axis_size("x"), lax.axis_size("zh")
    shares = call(
        combine_body, [((per_x, per_z, DH, rows), bf16)], count=2, flops=2 * D * DH * rows
    )(parts, w_out)
    received = [passed_along(block, DOM, o) for block, o in zip(chosen, offsets(REACH))]
    shares = lax.all_to_all(shares, "x", 0, 0)
    base = call(
        message_body,
        [((DH, rows), f32)],
        scratch=[pltpu.VMEM((rows // bound + directions, D, bound), bf16)],
        smem=(6, 7),
        count=10,
        flops=2 * D * rows * (4 * bound + DH),
    )(x_full, *received, tile_vals, tile_counts, tile_cols, w_msg.T, x_own)
    keep, send = call(
        fold_body, [((DH, rows), f32), ((DH, rows), bf16)], count=1, flops=D * rows
    )(shares)
    halves = lax.all_gather(send, "zh", axis=0, tiled=False)
    others = jnp.where(lax.axis_index("zh") == 0, halves[1], halves[0])
    return (base + keep + others.astype(f32)).astype(bf16).T


def solution(mesh):
    parts = Mesh(mesh.devices.reshape(PARTS), DOM + HEAD)
    placed = (
        P(DOM, HEAD),
        P(DOM, None, None, None),
        P(DOM),
        P(DOM, None),
        P(DOM, None, None),
        P(None, HEAD),
        P(None, None, HEAD),
        P(HEAD, None),
    )
    return jax.shard_map(local, mesh=parts, in_specs=placed, out_specs=P(DOM, HEAD), check_vma=False)
```
